256 devices in a mesh: seq: 16 (over x, z_lo), feat: 16 (over y, z_hi, core).
Axes of the slice: x: 4, y: 4, z: 8 (z_hi: 2, z_lo: 4; z = z_hi * 4 + z_lo), core: 2. Of those that a mesh axis runs over, the one named last changes fastest.
Arguments:
- tokens: bfloat16 [8192, 8192], P('seq', 'feat'), may hold values from -6 to 6
- butterfly: bfloat16 [16, 5, 512, 896], P('feat'), may hold values from -0.125 to 0.125
- low_in: bfloat16 [8192, 256], P('feat'), may hold values from -0.0625 to 0.0625
- low_out: bfloat16 [256, 14336], P(None, 'feat'), may hold values from -0.375 to 0.375
- cotangent: bfloat16 [8192, 14336], P('seq', 'feat'), may hold values from -6 to 6
Outputs:
- activated: bfloat16 [8192, 14336], P('seq', 'feat')
- tokens_grad: bfloat16 [8192, 8192], P('seq', 'feat')
- butterfly_grad: float32 [16, 5, 512, 896], P('feat', None, 'seq')
- low_in_grad: float32 [8192, 256], P('feat', 'seq')
- low_out_grad: float32 [256, 14336], P('seq', 'feat')
The draws below stay inside these ranges and needn't reach their ends.
All inputs are finite; a program needn't handle non-finite values.
Results may differ from the reference program's by a relative error of at most 0.0058.
Values may be sent and summed in bfloat16 or wider, within the bound.
No kernel may reach another device: no remote copies, remote signals or barrier semaphores. Data moves between devices by JAX's collectives and lax.ppermute only.
A program may use at most 128 MiB of HBM per device.

```python
import jax
import jax.numpy as jnp

BLOCKS = 16
BLOCK_WIDTH = 512
HIDDEN_BLOCK = 896
RANK = 256
MODEL_WIDTH = 8192
HIDDEN_SIZE = 14336
TOKENS = 8192


def steps_of(key, dims, shards, smallest, high):
    gain = 1.0
    for axis_at, blocks in shards:
        heights = jax.random.uniform(jax.random.fold_in(jax.random.fold_in(key, 6), axis_at), (blocks,), jnp.float32, smallest / len(shards), high / len(shards))
        gain = gain * jnp.repeat(jnp.exp(heights), dims[axis_at] // blocks).reshape((-1,) + (1,) * (len(dims) - 1 - axis_at))
    return gain


def centred(stream_key, shape, width, limit, split=(), dtype=jnp.bfloat16):
    factor_of = steps_of(stream_key, shape, split, -0.22, 0.18) if split else 1.0
    array = jax.random.normal(stream_key, shape, jnp.float32) * width * factor_of
    return jnp.minimum(jnp.maximum(array, -limit), limit).astype(dtype)


def setup_inputs(seed: int = 0) -> dict:
    arg_keys = jax.random.split(jax.random.key(seed), 6)
    return {
        "tokens": centred(arg_keys[0], (TOKENS, MODEL_WIDTH), 1.0, 6.0, ((0, 16), (1, 16))),
        "butterfly": centred(arg_keys[1], (BLOCKS, 5, BLOCK_WIDTH, HIDDEN_BLOCK), (5 * BLOCK_WIDTH) ** -0.5, 0.125, ((0, 16),)),
        "low_in": centred(arg_keys[2], (MODEL_WIDTH, RANK), MODEL_WIDTH ** -0.5, 0.0625, ((0, 16),)),
        "low_out": centred(arg_keys[3], (RANK, HIDDEN_SIZE), RANK ** -0.5, 0.375, ((1, 16),)),
        "cotangent": centred(arg_keys[4], (TOKENS, HIDDEN_SIZE), 1.0, 6.0, ((0, 16), (1, 16))),
    }


def gelu_tanh(values):
    return jax.nn.gelu(values, approximate=True)

def source_block(target, slot):
    if slot == 0:
        return target
    return target ^ 1 << slot - 1

def reference(tokens, butterfly, low_in, low_out, cotangent):
    blocks = tokens.reshape(TOKENS, BLOCKS, BLOCK_WIDTH)
    low_rank = jnp.dot(tokens, low_in, preferred_element_type=jnp.float32).astype(jnp.bfloat16)
    columns = []
    for target in range(BLOCKS):
        upper = low_out[:, target * HIDDEN_BLOCK:(target + 1) * HIDDEN_BLOCK]
        total = jnp.dot(low_rank, upper, preferred_element_type=jnp.float32)
        for slot in range(5):
            total = total + jnp.dot(blocks[:, source_block(target, slot)], butterfly[target, slot], preferred_element_type=jnp.float32)
        columns.append(total)
    pre = jnp.concatenate(columns, axis=1)
    activ, pullback = jax.vjp(gelu_tanh, pre)
    activated = activ.astype(jnp.bfloat16)
    grad_pre = pullback(cotangent.astype(jnp.float32))[0].astype(jnp.bfloat16)
    low_grad = jnp.dot(grad_pre, low_out.T, preferred_element_type=jnp.float32).astype(jnp.bfloat16)
    grad_blocks = grad_pre.reshape(TOKENS, BLOCKS, HIDDEN_BLOCK)
    pieces = []
    for source in range(BLOCKS):
        rows_in = low_in[source * BLOCK_WIDTH:(source + 1) * BLOCK_WIDTH]
        total = jnp.dot(low_grad, rows_in.T, preferred_element_type=jnp.float32)
        total = total + jnp.dot(grad_blocks[:, source], butterfly[source, 0].T, preferred_element_type=jnp.float32)
        for bit_level in range(4):
            target = source ^ 1 << bit_level
            total = total + jnp.dot(grad_blocks[:, target], butterfly[target, 1 + bit_level].T, preferred_element_type=jnp.float32)
        pieces.append(total)
    tokens_grad = jnp.concatenate(pieces, axis=1).astype(jnp.bfloat16)
    grads = []
    for target in range(BLOCKS):
        row_list = []
        for slot in range(5):
            row_list.append(jnp.dot(blocks[:, source_block(target, slot)].T, grad_blocks[:, target], preferred_element_type=jnp.float32))
        grads.append(jnp.stack(row_list, axis=0))
    butterfly_grad = jnp.stack(grads, axis=0)
    low_in_grad = jnp.dot(tokens.T, low_grad, preferred_element_type=jnp.float32)
    low_out_grad = jnp.dot(low_rank.T, grad_pre, preferred_element_type=jnp.float32)
    return (activated, tokens_grad, butterfly_grad, low_in_grad, low_out_grad)
```

```python
import jax
import jax.numpy as jnp
from jax import lax
from jax.sharding import Mesh
from jax.sharding import PartitionSpec as P

BF16 = jnp.bfloat16
F32 = jnp.float32
CHUNKS = (((0, 256), (256, 512)), ((512, 768), (768, 896)))


def flip(block, axis, mask):
    return lax.ppermute(block, axis, [(i, i ^ mask) for i in range(lax.axis_size(axis))])


def dot(a, b):
    return jnp.dot(a, b, preferred_element_type=F32)


def dot_nt(a, b):
    return lax.dot_general(a, b, (((1,), (1,)), ((), ())), preferred_element_type=F32)


def dot_tn(a, b):
    return lax.dot_general(a, b, (((0,), (0,)), ((), ())), preferred_element_type=F32)


def at(x, i):
    return lax.dynamic_index_in_dim(x, i, 0, keepdims=False)


def sum_over_feat(part):
    core = lax.axis_index("c")
    rows, width = part.shape
    halves = part.reshape(2, rows // 2, width)
    half = at(halves, core) + flip(at(halves, 1 - core), "c", 1)
    quarters = lax.all_to_all(half.reshape(4, rows // 8, width), "y", 0, 0, tiled=True)
    own = jnp.sum(quarters, axis=0)
    own = (own + flip(own, "zh", 1)).astype(BF16)
    half = lax.all_to_all(jnp.broadcast_to(own, (4, *own.shape)), "y", 0, 0, tiled=True)
    half = half.reshape(rows // 2, width)
    other = flip(half, "c", 1)
    first = core == 0
    return jnp.concatenate([jnp.where(first, half, other), jnp.where(first, other, half)], axis=0)


def take_z(rows, zl):
    width = rows.shape[1]
    main = lax.dynamic_slice_in_dim(rows[:640].reshape(5, 4, 32, width), zl, 1, 1).reshape(160, width)
    low = lax.dynamic_slice_in_dim(rows[640:].reshape(4, 16, width), zl, 1, 0).reshape(16, width)
    return jnp.concatenate([main, low], axis=0)


def sum_over_seq(rel, grads, columns, first, second):
    g = grads[:, columns[0] : columns[1]]
    width = columns[1] - columns[0]
    zl = lax.axis_index("zl")
    send = dot_tn(jnp.concatenate([rel[first], rel[2]], axis=1), g).astype(BF16)
    got = flip(send, "x", first).astype(F32).reshape(2, 704, width)
    keep = dot_tn(jnp.concatenate([rel[0], rel[second]], axis=1), g).reshape(2, 704, width)
    mine = keep[0] + got[0]
    got = flip((keep[1] + got[1]).astype(BF16), "x", second).astype(F32)
    mine = mine + got
    send = jnp.concatenate([take_z(mine, zl ^ 1), take_z(mine, zl ^ 3)], axis=0).astype(BF16)
    got = flip(send, "zl", 1).astype(F32)
    keep = take_z(mine, zl ^ 2) + got[176:]
    mine = take_z(mine, zl) + got[:176]
    return mine + flip(keep.astype(BF16), "zl", 2).astype(F32)


def gelu_and_slope(v):
    k = 0.7978845608028654
    cube = 0.044715
    t = jnp.tanh(k * (v + cube * v * v * v))
    half = 0.5 * (1.0 + t)
    return v * half, half + 0.5 * v * (1.0 - t * t) * (k * (1.0 + 3.0 * cube * v * v))


def local(tokens, butterfly, low_in, low_out, cotangent):
    x = lax.axis_index("x")
    weights = [butterfly[0, s] for s in range(5)]
    routes = (("c", 1), ("zh", 1), ("y", 1), ("y", 2))
    got = [None] * 4
    for s in (1, 3, 2, 0):
        got[s] = flip(tokens, *routes[s])
    blocks = [tokens] + got
    low_rank = sum_over_feat(dot(tokens, low_in))
    pre = dot(tokens, weights[0])
    for s in (1, 3, 4):
        pre = pre + dot(blocks[s], weights[s])
    pre = pre + dot(low_rank, low_out)
    pre = pre + dot(blocks[2], weights[2])
    value, slope = gelu_and_slope(pre)
    activated = value.astype(BF16)
    grads = (cotangent.astype(F32) * slope).astype(BF16)

    low_grad = sum_over_feat(dot_nt(grads, low_out))
    rel = []
    for r in range(4):
        place = x ^ r
        parts = [lax.dynamic_slice_in_dim(b, place * 128, 128, 1) for b in blocks]
        parts.append(lax.dynamic_slice_in_dim(low_rank, place * 64, 64, 1))
        rel.append(jnp.concatenate(parts, axis=1))
    lines = []
    for a, b in CHUNKS:
        lines.append(sum_over_seq(rel, grads, a, 1, 3))
        lines.append(sum_over_seq(rel, grads, b, 3, 1))
    lines = jnp.concatenate(lines, axis=1)
    butterfly_grad = lines[:160].reshape(1, 5, 32, -1)
    low_out_grad = lines[160:]

    back = dot_nt(grads, weights[0])
    for s in (1, 3, 2, 0):
        back = back + flip(dot_nt(grads, weights[1 + s]).astype(BF16), *routes[s]).astype(F32)
    tokens_grad = (back + dot_nt(low_grad, low_in)).astype(BF16)
    in_terms = dot_tn(low_grad, tokens).astype(BF16).reshape(16, 16, -1)
    in_terms = lax.all_to_all(in_terms, ("x", "zl"), 0, 0, tiled=True)
    low_in_grad = jnp.sum(in_terms.astype(F32), axis=0).T
    return activated, tokens_grad, butterfly_grad, low_in_grad, low_out_grad


def solution(mesh):
    fine = Mesh(mesh.devices.reshape(4, 4, 4, 2, 2), ("x", "zl", "y", "zh", "c"))
    seq, feat = ("x", "zl"), ("y", "zh", "c")
    return jax.shard_map(
        local,
        mesh=fine,
        in_specs=(
            P(seq, feat),
            P(feat, None, None, None),
            P(feat, None),
            P(None, feat),
            P(seq, feat),
        ),
        out_specs=(
            P(seq, feat),
            P(seq, feat),
            P(feat, None, seq, None),
            P(feat, seq),
            P(seq, feat),
        ),
        check_vma=False,
    )
```

```python
import jax
import jax.numpy as jnp
from jax import lax
from jax.experimental import pallas as pl
from jax.experimental.pallas import tpu as pltpu
from jax.sharding import Mesh
from jax.sharding import PartitionSpec as P

BF16 = jnp.bfloat16
F32 = jnp.float32
CHUNKS = (((0, 256), (256, 512)), ((512, 768), (768, 896)))
WAYS = ((1, 3), (3, 1))
EARLY = 384
VMEM = pl.BlockSpec(memory_space=pltpu.VMEM)
HBM = pl.BlockSpec(memory_space=pltpu.HBM)
SMEM = pl.BlockSpec(memory_space=pltpu.SMEM)


def flip(block, axis, mask):
    return lax.ppermute(block, axis, [(i, i ^ mask) for i in range(lax.axis_size(axis))])


def swap(blocks, axis):
    return lax.all_to_all(blocks, axis, 0, 0, tiled=True)


def dot(a, b):
    return jnp.dot(a, b, preferred_element_type=F32)


def dot_nt(a, b):
    return lax.dot_general(a, b, (((1,), (1,)), ((), ())), preferred_element_type=F32)


def dot_tn(a, b):
    return lax.dot_general(a, b, (((0,), (0,)), ((), ())), preferred_element_type=F32)


def at(x, i):
    return lax.dynamic_index_in_dim(x, i, 0, keepdims=False)


def kernel(body, outs, specs, *args, scratch=()):
    return pl.pallas_call(
        body,
        in_specs=specs,
        out_specs=[VMEM] * len(outs),
        out_shape=[jax.ShapeDtypeStruct(*o) for o in outs],
        scratch_shapes=list(scratch),
        compiler_params=pltpu.CompilerParams(vmem_limit_bytes=24 << 20),
    )(*args)


def in_hbm(x):
    return pltpu.with_memory_space_constraint(x, pltpu.HBM)


def fetch(pairs, sems):
    copies = [pltpu.make_async_copy(src, dst, sems.at[k]) for k, (src, dst) in enumerate(pairs)]
    for c in copies:
        c.start()
    return copies


def forward_sum(table, blocks, slots, butterfly):
    n = len(slots)

    def body(table, *refs):
        weights, out, turned = refs[n:]
        for i in range(2):
            rows = slice(256 * i, 256 * i + 256)
            total = dot(refs[0][rows], weights[0, slots[0]])
            for k in range(1, n):
                total = total + dot(refs[k][rows], weights[0, slots[k]])
            out[rows] = total
        for r in range(4):
            column = pl.multiple_of(table[r] * 128, 128)
            for k in range(n):
                turned[r, 128 * k : 128 * k + 128] = refs[k][:, pl.ds(column, 128)].T

    outs = [((512, 896), F32), ((4, EARLY, 512), BF16)]
    return kernel(body, outs, [SMEM] + [VMEM] * (n + 1), table, *blocks, butterfly)


def gelu_and_slope(v):
    k = 0.7978845608028654
    cube = 0.044715
    t = jnp.tanh(k * (v + cube * v * v * v))
    half = 0.5 * (1.0 + t)
    return v * half, half + 0.5 * v * (1.0 - t * t) * (k * (1.0 + 3.0 * cube * v * v))


def forward_end(table, partial, far, across, butterfly, low_rank, low_out, cotangent):
    def body(table, part, far, across, weights, low, up, cot, act, grad, back, turned):
        for i in range(2):
            rows = slice(256 * i, 256 * i + 256)
            pre = part[rows] + dot(far[rows], weights[0, 4]) + dot(low[table[4 + i]], up[...])
            pre = pre + dot(across[rows], weights[0, 2])
            value, slope = gelu_and_slope(pre)
            act[rows] = value.astype(BF16)
            grads = (cot[rows].astype(F32) * slope).astype(BF16)
            grad[rows] = grads
            back[rows] = dot_nt(grads, up[...])
        for r in range(4):
            place = table[r]
            column = pl.multiple_of(place * 128, 128)
            turned[r, :128] = far[:, pl.ds(column, 128)].T
            turned[r, 128:256] = across[:, pl.ds(column, 128)].T
            column = pl.multiple_of((place // 2) * 128, 128)
            block = jnp.concatenate([low[table[4], :, pl.ds(column, 128)], low[table[5], :, pl.ds(column, 128)]], axis=0)
            block = block.T
            turned[r, 256:] = jnp.where(place % 2 == 0, block[:64], block[64:])

    outs = [((512, 896), BF16), ((512, 896), BF16), ((512, 256), F32), ((4, 704 - EARLY, 512), BF16)]
    args = (table, partial, far, across, butterfly, low_rank, low_out, cotangent)
    return kernel(body, outs, [SMEM] + [VMEM] * 7, *args)


def back_terms(grads, butterfly, slots, types):
    def body(g, weights, *outs):
        for k, s in enumerate(slots):
            outs[k][...] = dot_nt(g[...], weights[0, s]).astype(types[k])

    return kernel(body, [((512, 512), t) for t in types], [VMEM] * 2, grads, butterfly)


def lines(early, late, r, grads):
    return dot(early[r], grads), dot(late[r], grads)


def lines_to_send(order, early, late, grads, columns):
    width = columns[1] - columns[0]

    def body(early, late, grads, out):
        g = grads[:, columns[0] : columns[1]]
        for k, r in enumerate(order):
            a, b = lines(early, late, r, g)
            out[k, :EARLY] = a.astype(BF16)
            out[k, EARLY:] = b.astype(BF16)

    return kernel(body, [((2, 704, width), BF16)], [VMEM] * 3, early, late, grads)[0]


def lines_to_pass(far, early, late, grads, columns, got):
    width = columns[1] - columns[0]

    def body(early, late, grads, got, send):
        a, b = lines(early, late, far, grads[:, columns[0] : columns[1]])
        send[:EARLY] = (a + got[1, :EARLY].astype(F32)).astype(BF16)
        send[EARLY:] = (b + got[1, EARLY:].astype(F32)).astype(BF16)

    return kernel(body, [((704, width), BF16)], [VMEM] * 4, early, late, grads, got)[0]


def lines_of_place(table, early, late, grads, chunk, near, far):
    first = chunk[0][0]
    width = chunk[-1][1] - first

    def body(table, early, late_hbm, grads, near_a, near_b, far_a, far_b, send, keep, mine, space, late, sem, *got):
        taken, sems = got[:4], got[4]
        first_copy = fetch([(late_hbm.at[0], late)], sem)
        sources = (near_a.at[0], far_a, near_b.at[0], far_b)
        copies = fetch(list(zip(sources, taken)), sems)
        first_copy[0].wait()
        for h, (start, end) in enumerate(chunk):
            copies[2 * h].wait()
            copies[2 * h + 1].wait()
            n, f = taken[2 * h], taken[2 * h + 1]
            g = grads[:, start:end]
            to = slice(start - first, end - first)
            space[:EARLY, to] = dot(early[0], g) + n[:EARLY].astype(F32) + f[:EARLY].astype(F32)
            space[EARLY:, to] = dot(late[...], g) + n[EARLY:].astype(F32) + f[EARLY:].astype(F32)
        for r, out, base in ((1, send, 0), (3, send, 176), (2, keep, 0), (0, mine, 0)):
            place = table[8 + r]
            for s in range(5):
                rows = space[pl.ds(pl.multiple_of(128 * s + 32 * place, 32), 32)]
                out[base + 32 * s : base + 32 * s + 32] = rows.astype(out.dtype)
            rows = space[pl.ds(pl.multiple_of(640 + 16 * place, 16), 16)]
            out[base + 160 : base + 176] = rows.astype(out.dtype)

    outs = [((352, width), BF16), ((176, width), F32), ((176, width), F32)]
    args = (table, early, in_hbm(late), grads, *[in_hbm(v) for v in (*near, *far)])
    one = pltpu.SemaphoreType.DMA((1,))
    scratch = [pltpu.VMEM((704, width), F32), pltpu.VMEM((704 - EARLY, 512), BF16), one]
    for start, end in chunk:
        scratch += [pltpu.VMEM((704, end - start), BF16)] * 2
    scratch.append(pltpu.SemaphoreType.DMA((4,)))
    specs = [SMEM, VMEM, HBM, VMEM] + [HBM] * 4
    return kernel(body, outs, specs, *args, scratch=scratch)


def steps(tokens, butterfly, low_in, low_out, cotangent):
    x, zl, core = lax.axis_index("x"), lax.axis_index("zl"), lax.axis_index("c")
    places = jnp.repeat(jnp.stack([x, core, zl]), 4)
    table = jnp.array([0, 1, 2, 3, 0, 1, 0, 0, 0, 1, 2, 3], jnp.int32) ^ places.astype(jnp.int32)

    def sum_over_feat(part, kept):
        halves = part.reshape(2, 256, 256)
        own = at(halves, core) + flip(at(halves, 1 - core), "c", 1)
        for axis, mask in (("zh", 1), ("y", 1), ("y", 2)):
            own = own + flip(own.astype(kept), axis, mask).astype(F32)
        half = own.astype(BF16)[None]
        return jnp.concatenate([half, flip(half, "c", 1)], axis=0)

    low_rank = sum_over_feat(dot(tokens, low_in), BF16)
    near_block = flip(tokens, "y", 1)
    across = flip(tokens, "zh", 1)
    core_block = flip(tokens, "c", 1)
    far_block = flip(tokens, "y", 2)
    partial, early = forward_sum(table, [tokens, core_block, near_block], (0, 1, 3), butterfly)
    activated, grads, low_back, late = forward_end(
        table, partial, far_block, across, butterfly, low_rank, low_out, cotangent
    )

    got = {}
    for n, chunk in enumerate(CHUNKS):
        for h, columns in enumerate(chunk):
            near = WAYS[h][0]
            send = lines_to_send((near, 2), early, late, grads, columns)
            got[n, h] = flip(send, "x", near)

    low = sum_over_feat(low_back, BF16)
    (zh_term,) = back_terms(grads, butterfly, (2,), (BF16,))
    far_term, near_term, core_term, own_term = back_terms(grads, butterfly, (4, 3, 1, 0), (BF16, BF16, BF16, F32))
    zh_got = flip(zh_term, "zh", 1)
    near_got = flip(near_term, "y", 1)
    core_got = flip(core_term, "c", 1)
    far_got = flip(far_term, "y", 2)
    low_grad = jnp.where(core == 0, low, low[::-1]).reshape(512, 256)
    in_terms = dot_tn(low_grad, tokens).astype(BF16).reshape(16, 16, -1)
    in_terms = swap(in_terms, ("x", "zl")).astype(F32)
    low_in_grad = jnp.sum(in_terms, axis=0).T

    out = []
    for n, chunk in enumerate(CHUNKS):
        near, far = [], []
        for h, columns in enumerate(chunk):
            send = lines_to_pass(WAYS[h][1], early, late, grads, columns, got[n, h])
            near.append(got[n, h])
            far.append(flip(send, "x", WAYS[h][1]))
        send, keep, mine = lines_of_place(table, early, late, grads, chunk, near, far)
        back = flip(send, "zl", 1)
        send = (keep + back[176:].astype(F32)).astype(BF16)
        out.append(mine + back[:176].astype(F32) + flip(send, "zl", 2).astype(F32))
    out = jnp.concatenate(out, axis=1)
    slots = out[:160].reshape(5, 32, -1)
    butterfly_grad = jnp.stack([slots[0], slots[1], slots[4], slots[2], slots[3]])[None]
    low_out_grad = out[160:]

    total = own_term + zh_got.astype(F32)
    for term in (near_got, core_got, far_got):
        total = total + term.astype(F32)
    tokens_grad = (total + dot_nt(low_grad, low_in)).astype(BF16)
    return activated, tokens_grad, butterfly_grad, low_in_grad, low_out_grad


def solution(mesh):
    fine = Mesh(mesh.devices.reshape(4, 4, 4, 2, 2), ("x", "zl", "y", "zh", "c"))
    seq, feat = ("x", "zl"), ("y", "zh", "c")
    return jax.shard_map(
        steps,
        mesh=fine,
        in_specs=(
            P(seq, feat),
            P(feat, None, None, None),
            P(feat, None),
            P(None, feat),
            P(seq, feat),
        ),
        out_specs=(
            P(seq, feat),
            P(seq, feat),
            P(feat, None, seq, None),
            P(feat, seq),
            P(seq, feat),
        ),
        check_vma=False,
    )
```
